256 devices in a mesh: prow: 32 (over z_hi, y, x), pcol: 8 (over z_lo, core).
Axes of the slice: x: 4, y: 4, z: 8 (z_hi: 2, z_lo: 4; z = z_hi * 4 + z_lo), core: 2. Of those that a mesh axis runs over, the one named last changes fastest.
Arguments:
- design: float32 [1024, 32768], P('pcol', 'prow'), may hold values from -0.1875 to 0.1875
- damping: float32 [512], replicated, may hold values from 0.1 to 2
Outputs:
- factored: float32 [32768, 8192], P('prow', 'pcol')
The draws below stay inside these ranges and needn't reach their ends.
All inputs are finite; a program needn't handle non-finite values.
Results may differ from the reference program's by a relative error of at most 0.00011.
Values sent between devices are 32-bit elements; how exact they have to be, the bound alone decides.
No kernel may reach another device: no remote copies, remote signals or barrier semaphores. Data moves between devices by JAX's collectives and lax.ppermute only.
A program may use at most 128 MiB of HBM per device.

```python
import math
import jax
import jax.numpy as jnp
from jax import lax

BLOCK = 512
OBS = 1024
PARAMS = 32768
SLAB = 8192


def block_levels(rng, dims, shards, smallest, top_value):
    gain = 1.0
    for dim, parts in shards:
        steps = jax.random.uniform(jax.random.fold_in(jax.random.fold_in(rng, 6), dim), (parts,), jnp.float32, smallest / len(shards), top_value / len(shards))
        gain = gain * jnp.repeat(jnp.exp(steps), dims[dim] // parts).reshape((-1,) + (1,) * (len(dims) - 1 - dim))
    return gain


def gaussian(rng, extent, spread, bound, split=(), held_as=jnp.bfloat16):
    factor_of = block_levels(rng, extent, split, -0.22, 0.18) if split else 1.0
    drawn = jax.random.normal(rng, extent, jnp.float32) * spread * factor_of
    return jnp.minimum(jnp.maximum(drawn, -bound), bound).astype(held_as)


def setup_inputs(seed: int = 0) -> dict:
    key_list = jax.random.split(jax.random.key(seed), 3)
    return {
        "design": gaussian(key_list[0], (OBS, PARAMS), OBS ** -0.5, 0.1875, ((0, 8), (1, 32)), jnp.float32),
        "damping": jnp.clip(jnp.exp(jax.random.uniform(key_list[1], (BLOCK,), jnp.float32, math.log(0.1), math.log(2.0))), 0.1, 2.0),
    }


def reference(design, damping):
    gram = jnp.dot(design.T.astype(jnp.float32), design[:, :SLAB].astype(jnp.float32), precision=lax.Precision.HIGHEST, preferred_element_type=jnp.float32)
    diagonal_index = jnp.arange(BLOCK, dtype=jnp.int32)
    shifted = gram.at[diagonal_index, diagonal_index].add(damping)
    diagonal_factor = jnp.linalg.cholesky(shifted[:BLOCK, :BLOCK])
    panel_full = jax.scipy.linalg.solve_triangular(diagonal_factor, shifted[:, :BLOCK].T, lower=True).T
    trailing = shifted[:, BLOCK:] - jnp.dot(panel_full.astype(jnp.float32), panel_full[BLOCK:SLAB].T.astype(jnp.float32), precision=lax.Precision.HIGHEST, preferred_element_type=jnp.float32)
    return jnp.concatenate([panel_full, trailing], axis=1)
```

```python
import jax
import jax.numpy as jnp
from jax import lax
from jax.sharding import Mesh
from jax.sharding import PartitionSpec as P

BLOCK = 512
AXES = ("zh", "y", "x", "zl", "core")
SIZES = (2, 4, 4, 4, 2)
ROW = ("zh", "y", "x")
COL = ("zl", "core")


def device_id(zh, y, x, zl, core):
    return (((zh * 4 + y) * 4 + x) * 4 + zl) * 2 + core


def ring(n, shift):
    return [(i, (i + shift) % n) for i in range(n)]


def spread_lead(value):
    columns = [(zl, core) for zl in range(4) for core in range(2)]

    def stage(value, moves):
        received = [
            lax.ppermute(value, AXES, [(device_id(*s, *c), device_id(*t, *c)) for s, t in move for c in columns])
            for move in moves
        ]
        for piece in received:
            value = value + piece
        return value

    value = stage(value, [[((0, 0, 0), (0, 0, x))] for x in (1, 3, 2)])
    value = stage(value, [[((0, 0, x), (0, y, x)) for x in range(4)] for y in (1, 3, 2)])
    return stage(value, [[((0, y, x), (1, y, x)) for y in range(4) for x in range(4)]])


def gather_lead(value):
    mine = jnp.stack([value] + [lax.ppermute(value, "zl", ring(4, k)) for k in (1, 2, 3)])
    other = lax.ppermute(mine, "core", ring(2, 1))
    both = jnp.stack([mine, other])
    zl, core = lax.axis_index("zl"), lax.axis_index("core")
    pieces = []
    for k in range(8):
        which = (core + k) % 2
        step = (zl - k // 2 + 4) % 4
        pieces.append(lax.dynamic_slice(both, (which, step, 0, 0), (1, 1, *value.shape)).reshape(value.shape))
    return jnp.concatenate(pieces)


def scatter_columns(design):
    half = design.shape[0] // 2
    mine = 0.0
    for zh in range(2):
        for j in range(2):
            pairs = []
            for c in range(8):
                for k in range(8):
                    p = 2 * k + j
                    pairs.append(
                        (device_id(0, c // 4, c % 4, k // 2, k % 2), device_id(zh, p // 4, p % 4, c // 2, c % 2))
                    )
            mine = mine + lax.ppermute(design[j * half : (j + 1) * half], AXES, pairs)
    return mine


def mm(a, b, dims, precision=lax.Precision.HIGH):
    return lax.dot_general(a, b, (dims, ((), ())), precision=precision, preferred_element_type=jnp.float32)


def per_device(design, damping):
    row = lax.axis_index(ROW)
    col = lax.axis_index(COL)
    is_root = row == 0
    lead_mine = jnp.where(is_root, design[:, :BLOCK], 0.0)
    lead = gather_lead(spread_lead(lead_mine))
    rows = lax.all_gather(design, COL, tiled=True)
    columns = lax.all_gather(scatter_columns(design), ("y", "x"), tiled=True)

    highest = lax.Precision.HIGHEST
    lead_gram = mm(lead, lead, ((0,), (0,)), highest) + jnp.diag(damping)
    factor = jnp.linalg.cholesky(lead_gram)
    inverse = jax.scipy.linalg.solve_triangular(factor, jnp.eye(BLOCK, dtype=jnp.float32), lower=True)
    white = mm(lead, inverse, ((1,), (1,)), highest)
    other = mm(white, columns, ((0,), (0,)))
    projected = columns - mm(white, other, ((1,), (0,)))
    is_panel = (col == 0) & (jnp.arange(columns.shape[1]) < BLOCK)
    width = columns.shape[1] - BLOCK
    right = jnp.where(is_panel[None, :], jnp.pad(white, ((0, 0), (0, width))), projected)
    out = mm(rows, right, ((0,), (0,)))
    correction = jnp.where(
        is_panel[None, :], jnp.pad(inverse.T, ((0, 0), (0, width))), -mm(inverse, other, ((0,), (0,)))
    )
    correction = jnp.where(is_root, damping[:, None] * correction, 0.0)
    return out + jnp.pad(correction, ((0, width), (0, 0)))


def solution(mesh):
    fine = Mesh(mesh.devices.reshape(SIZES), AXES)
    return jax.shard_map(per_device, mesh=fine, in_specs=(P(COL, ROW), P()), out_specs=P(ROW, COL), check_vma=False)
```

```python
import jax
import jax.numpy as jnp
from jax import lax
from jax.experimental import pallas as pl
from jax.experimental.pallas import tpu as pltpu
from jax.sharding import Mesh
from jax.sharding import PartitionSpec as P

BLOCK = 512
SUB = 128
TILE = 256
AXES = ("zh", "y", "x", "zl", "core")
SIZES = (2, 4, 4, 4, 2)
ROW = ("zh", "y", "x")
COL = ("zl", "core")


def device_id(zh, y, x, zl, core):
    return (((zh * 4 + y) * 4 + x) * 4 + zl) * 2 + core


def ring(n, shift):
    return [(i, (i + shift) % n) for i in range(n)]


def spread_lead(value):
    columns = [(zl, core) for zl in range(4) for core in range(2)]

    def stage(value, moves):
        received = [
            lax.ppermute(value, AXES, [(device_id(*s, *c), device_id(*t, *c)) for s, t in move for c in columns])
            for move in moves
        ]
        for piece in received:
            value = value + piece
        return value

    value = stage(value, [[((0, 0, 0), (0, 0, x))] for x in (1, 3, 2)])
    value = stage(value, [[((0, 0, x), (0, y, x)) for x in range(4)] for y in (1, 3, 2)])
    return stage(value, [[((0, y, x), (1, y, x)) for y in range(4) for x in range(4)]])


def gather_lead(value):
    mine = jnp.stack([value] + [lax.ppermute(value, "zl", ring(4, k)) for k in (1, 2, 3)])
    other = lax.ppermute(mine, "core", ring(2, 1))
    zl, core = lax.axis_index("zl"), lax.axis_index("core")
    chip = (zl - jnp.arange(4) + 4) & 3
    return mine, other, jnp.concatenate([2 * chip + core, 2 * chip + 1 - core]).astype(jnp.int32)


def scatter_columns(design):
    half = design.shape[0] // 2
    mine = 0.0
    for zh in range(2):
        for j in range(2):
            pairs = []
            for c in range(8):
                for k in range(8):
                    p = 2 * k + j
                    pairs.append(
                        (device_id(0, c // 4, c % 4, k // 2, k % 2), device_id(zh, p // 4, p % 4, c // 2, c % 2))
                    )
            mine = mine + lax.ppermute(design[j * half : (j + 1) * half], AXES, pairs)
    return mine


def dot(a, b, dims, precision=None):
    return lax.dot_general(a, b, (dims, ((), ())), precision=precision, preferred_element_type=jnp.float32)


def split(a):
    high = a.astype(jnp.bfloat16)
    return high, (a - high.astype(jnp.float32)).astype(jnp.bfloat16)


def dot3(a, b, dims):
    return dot(a[0], b[0], dims) + (dot(a[0], b[1], dims) + dot(a[1], b[0], dims))


def eliminate(m_ref):
    lane = lax.broadcasted_iota(jnp.int32, (8, SUB), 1)
    sub = lax.broadcasted_iota(jnp.int32, (8, SUB), 0)
    for o in range(0, SUB, 8):
        left = [jnp.broadcast_to(m_ref[o + i : o + i + 1, :SUB], (8, SUB)) for i in range(8)]
        right = [jnp.broadcast_to(m_ref[o + i : o + i + 1, SUB:], (8, SUB)) for i in range(8)]
        e = {
            (i, j): jnp.broadcast_to(left[i][:, o + j : o + j + 1], (8, SUB)) for i in range(8) for j in range(i, 8)
        }
        strip_left = jnp.zeros((8, SUB), jnp.float32)
        strip_right = strip_left
        for i in range(8):
            r = lax.rsqrt(e[i, i])
            for j in range(i + 1, 8):
                e[i, j] = e[i, j] * r
            for j in range(i + 1, 8):
                for k in range(j, 8):
                    e[j, k] = e[j, k] - e[i, j] * e[i, k]
            a, b = left[i] * r, right[i] * r
            for j in range(i + 1, 8):
                left[j] = left[j] - e[i, j] * a
                right[j] = right[j] - e[i, j] * b
            strip_left = jnp.where(sub == i, a, strip_left)
            strip_right = jnp.where(sub == i, b, strip_right)
        m_ref[o : o + 8, :SUB] = strip_left
        m_ref[o : o + 8, SUB:] = strip_right
        if o + 8 < SUB:
            masked = jnp.where(lane >= o + 8, strip_left, 0.0)
            strip = jnp.concatenate([strip_left, strip_right], axis=1)
            update = dot(masked, strip, ((0,), (0,)), lax.Precision.HIGHEST)
            m_ref[o + 8 :, :] = m_ref[o + 8 :, :] - update[o + 8 :, :]


def lead_kernel(place_ref, mine_ref, other_ref, damping_ref, white_ref, inverse_ref, g_ref, m_ref):
    highest = lax.Precision.HIGHEST
    pieces = mine_ref.shape[0]
    depth = mine_ref.shape[1]
    both = [ref[...].reshape(pieces * depth, BLOCK) for ref in (mine_ref, other_ref)]
    same = lax.broadcasted_iota(jnp.int32, (BLOCK, BLOCK), 0) == lax.broadcasted_iota(jnp.int32, (BLOCK, BLOCK), 1)
    gram = dot(both[0], both[0], ((0,), (0,)), highest) + dot(both[1], both[1], ((0,), (0,)), highest)
    g_ref[:, :BLOCK] = gram + jnp.where(same, damping_ref[...], 0.0)
    g_ref[:, BLOCK:] = jnp.where(same, 1.0, 0.0)

    def step(p, carry):
        start = pl.multiple_of(p * SUB, SUB)
        m_ref[:, :SUB] = g_ref[pl.ds(start, SUB), pl.ds(start, SUB)]
        m_ref[:, SUB:] = jnp.where(same[:SUB, :SUB], 1.0, 0.0)
        eliminate(m_ref)
        inverse = m_ref[:, SUB:]
        for q in range(BLOCK // SUB):

            @pl.when(p == q)
            def _():
                lo, hi = q * SUB, (q + 1) * SUB
                strip = dot(inverse, g_ref[lo:hi, hi : hi + BLOCK], ((1,), (0,)), highest)
                g_ref[lo:hi, hi : hi + BLOCK] = strip
                if hi < BLOCK:
                    g_ref[hi:BLOCK, hi : hi + BLOCK] = g_ref[hi:BLOCK, hi : hi + BLOCK] - dot(
                        strip[:, : BLOCK - hi], strip, ((0,), (0,)), highest
                    )

        return carry

    lax.fori_loop(0, BLOCK // SUB, step, 0)
    inverse = g_ref[:, BLOCK:]
    inverse_ref[...] = inverse * damping_ref[...]
    pair = split(inverse)
    for h, ref in enumerate((mine_ref, other_ref)):
        for i in range(pieces):
            start = pl.multiple_of(place_ref[h * pieces + i] * depth, depth)
            white_ref[pl.ds(start, depth), :] = dot3(split(ref[i]), pair, ((1,), (1,)))


def lead_call(mine, other, place, damping):
    vmem = pl.BlockSpec(memory_space=pltpu.VMEM)
    rows = 2 * mine.shape[0] * mine.shape[1]
    return pl.pallas_call(
        lead_kernel,
        out_shape=(jax.ShapeDtypeStruct((rows, BLOCK), jnp.float32), jax.ShapeDtypeStruct((BLOCK, BLOCK), jnp.float32)),
        in_specs=[pl.BlockSpec(memory_space=pltpu.SMEM), vmem, vmem, vmem],
        out_specs=(vmem, vmem),
        scratch_shapes=[pltpu.VMEM((BLOCK, 2 * BLOCK), jnp.float32), pltpu.VMEM((SUB, 2 * SUB), jnp.float32)],
        name="lead",
    )(place, mine, other, damping.reshape(1, BLOCK))


def apply_kernel(where_ref, rows_ref, columns_ref, white_ref, inverse_ref, out_ref, wh, wl, vh, vl, rh, rl):
    t = pl.program_id(0)
    tiles = out_ref.shape[1] // TILE
    is_root = where_ref[0] == 0
    has_panel = where_ref[1] == 0
    white = (wh, wl)

    def put(refs, value, index):
        refs[0][index], refs[1][index] = split(value)

    def get(refs, index=...):
        return refs[0][index], refs[1][index]

    @pl.when(t == 0)
    def _():
        put(white, white_ref[...], ...)

    for j in range(tiles):

        @pl.when(t == j)
        def _():
            here = (slice(None), slice(j * TILE, (j + 1) * TILE))

            def trailing():
                block = columns_ref[...]
                put((vh, vl), dot3(get(white), split(block), ((0,), (0,))), here)
                put((rh, rl), block - dot3(get(white), get((vh, vl), here), ((1,), (0,))), here)

            if j * TILE < BLOCK:
                pl.when(jnp.logical_not(has_panel))(trailing)

                @pl.when(has_panel)
                def _():
                    row = lax.broadcasted_iota(jnp.int32, (BLOCK, TILE), 0)
                    column = lax.broadcasted_iota(jnp.int32, (BLOCK, TILE), 1) + j * TILE
                    put((vh, vl), jnp.where(row == column, -1.0, 0.0), here)
                    rh[here], rl[here] = get(white, here)
            else:
                trailing()

    @pl.when(t >= tiles)
    def _():
        out_ref[...] = dot3(split(rows_ref[...]), get((rh, rl)), ((0,), (0,)))

    for i in range(BLOCK // TILE):

        @pl.when((t == tiles + i) & is_root)
        def _():
            scaled = split(inverse_ref[:, i * TILE : (i + 1) * TILE])
            out_ref[...] = out_ref[...] - dot3(scaled, get((vh, vl)), ((0,), (0,)))


def apply_call(where, rows, columns, white, inverse):
    depth, size = rows.shape
    tiles = size // TILE
    bf16 = jnp.bfloat16
    grid_spec = pltpu.PrefetchScalarGridSpec(
        num_scalar_prefetch=1,
        grid=(2 * tiles,),
        in_specs=[
            pl.BlockSpec((depth, TILE), lambda t, w: (0, jnp.maximum(t - tiles, 0))),
            pl.BlockSpec((depth, TILE), lambda t, w: (0, jnp.minimum(t, tiles - 1))),
            pl.BlockSpec((depth, BLOCK), lambda t, w: (0, 0)),
            pl.BlockSpec((BLOCK, BLOCK), lambda t, w: (0, 0)),
        ],
        out_specs=pl.BlockSpec((TILE, size), lambda t, w: (jnp.maximum(t - tiles, 0), 0)),
        scratch_shapes=[pltpu.VMEM((depth, BLOCK), bf16)] * 2
        + [pltpu.VMEM((BLOCK, size), bf16)] * 2
        + [pltpu.VMEM((depth, size), bf16)] * 2,
    )
    return pl.pallas_call(
        apply_kernel, grid_spec=grid_spec, out_shape=jax.ShapeDtypeStruct((size, size), jnp.float32), name="apply"
    )(where, rows, columns, white, inverse)


def per_device(design, damping):
    row = lax.axis_index(ROW)
    col = lax.axis_index(COL)
    mine, other, place = gather_lead(spread_lead(jnp.where(row == 0, design[:, :BLOCK], 0.0)))
    rows = lax.all_gather(design, COL, tiled=True)
    columns = lax.all_gather(scatter_columns(design), ("y", "x"), tiled=True)
    white, inverse = lead_call(mine, other, place, damping)
    return apply_call(jnp.stack([row, col]).astype(jnp.int32), rows, columns, white, inverse)


def solution(mesh):
    fine = Mesh(mesh.devices.reshape(SIZES), AXES)
    return jax.shard_map(per_device, mesh=fine, in_specs=(P(COL, ROW), P()), out_specs=P(ROW, COL), check_vma=False)
```

```python
import functools
import itertools

import jax
import jax.numpy as jnp
from jax import lax
from jax.experimental import pallas as pl
from jax.experimental.pallas import tpu as pltpu
from jax.sharding import Mesh
from jax.sharding import PartitionSpec as P


BLOCK = 512
SUB = 128
TILE = 256
PIECES = 8
LEAD_SHIFTS = (0, 1, 3, 2)
ROW_SHIFTS = (0, 1, 2, 3)
AXES = ("zh", "y", "x", "zl", "core")
SIZES = (2, 4, 4, 4, 2)
ROW = ("zh", "y", "x")
COL = ("zl", "core")


def device_id(zh, y, x, zl, core):
    return (((zh * 4 + y) * 4 + x) * 4 + zl) * 2 + core


def ring(n, shift):
    return [(i, (i + shift) % n) for i in range(n)]


def permute_rows(value, moves):
    columns = [(zl, core) for zl in range(4) for core in range(2)]
    values = value if isinstance(value, list) else [value] * len(moves)
    return [
        lax.ppermute(values[i], AXES, [(device_id(*s, *c), device_id(*t, *c)) for s, t in move for c in columns])
        for i, move in enumerate(moves)
    ]


def total(values):
    return functools.reduce(jnp.add, values)


def spread_lead(design, is_root):
    quarters = jnp.split(jnp.where(is_root, design[:, :BLOCK], 0.0), 4)
    others = (1, 3, 2)
    mine = quarters[0] + total(permute_rows([quarters[x] for x in others], [[((0, 0, 0), (0, 0, x))] for x in others]))
    mine = mine + total(permute_rows(mine, [[((0, 0, x), (0, y, x)) for x in range(4)] for y in others]))
    mine = mine + total(permute_rows(mine, [[((0, y, x), (1, y, x)) for y in range(4) for x in range(4)]]))
    mine = jnp.concatenate([mine] + [lax.ppermute(mine, "x", ring(4, k)) for k in LEAD_SHIFTS[1:]])
    line = [mine]
    for k in LEAD_SHIFTS[1:]:
        pairs = []
        for y, x, z, core in itertools.product(range(4), range(4), range(8), range(2)):
            to = (z + (-k if k == 2 and core else k)) % 8
            pairs.append((device_id(z // 4, y, x, z % 4, core), device_id(to // 4, y, x, to % 4, core)))
        line.append(lax.ppermute(mine, AXES, pairs))
    return swap_cores(line)


def swap_cores(line):
    return line + [lax.ppermute(piece, "core", ring(2, 1)) for piece in line]


def gather_rows(design):
    return swap_cores([design] + [lax.ppermute(design, "zl", ring(4, k)) for k in ROW_SHIFTS[1:]])


def places(shifts):
    zl, core = lax.axis_index("zl"), lax.axis_index("core")
    chip = (zl + 4 - jnp.array(shifts, jnp.int32)) & 3
    return jnp.concatenate([2 * chip + core, 2 * chip + 1 - core])


def inverse_of(place):
    index = jnp.arange(PIECES, dtype=jnp.int32)
    return jnp.sum(jnp.where(place[None, :] == index[:, None], index[None, :], 0), axis=1)


def scatter_columns(design):
    halves = jnp.split(design, 2)
    planes = []
    for j in range(2):
        pairs = []
        for c, k in itertools.product(range(8), range(8)):
            p = (2 * (k + c) + j) % 16
            pairs.append((device_id(0, c // 4, c % 4, k // 2, k % 2), device_id(0, p // 4, p % 4, k // 2, k % 2)))
        planes.append(lax.ppermute(halves[j], AXES, pairs))
    mine = planes[0] + planes[1]
    lines = []
    for zh in range(2):
        pairs = []
        for p, k in itertools.product(range(16), range(8)):
            c = (p // 2 - k) % 8
            pairs.append((device_id(0, p // 4, p % 4, k // 2, k % 2), device_id(zh, p // 4, p % 4, c // 2, c % 2)))
        lines.append(lax.ppermute(mine, AXES, pairs))
    return lines[0] + lines[1]


def dot(a, b, dims, precision=None):
    return lax.dot_general(a, b, (dims, ((), ())), precision=precision, preferred_element_type=jnp.float32)


def split(a):
    high = a.astype(jnp.bfloat16)
    return high, (a - high.astype(jnp.float32)).astype(jnp.bfloat16)


def dot3(a, b, dims):
    return dot(a[0], b[0], dims) + (dot(a[0], b[1], dims) + dot(a[1], b[0], dims))


def eliminate(m_ref):
    lane = lax.broadcasted_iota(jnp.int32, (8, SUB), 1)
    sub = lax.broadcasted_iota(jnp.int32, (8, SUB), 0)
    for o in range(0, SUB, 8):
        left = [jnp.broadcast_to(m_ref[o + i : o + i + 1, :SUB], (8, SUB)) for i in range(8)]
        right = [jnp.broadcast_to(m_ref[o + i : o + i + 1, SUB:], (8, SUB)) for i in range(8)]
        e = {
            (i, j): jnp.broadcast_to(left[i][:, o + j : o + j + 1], (8, SUB)) for i in range(8) for j in range(i, 8)
        }
        strip_left = jnp.zeros((8, SUB), jnp.float32)
        strip_right = strip_left
        for i in range(8):
            r = lax.rsqrt(e[i, i])
            for j in range(i + 1, 8):
                e[i, j] = e[i, j] * r
            for j in range(i + 1, 8):
                for k in range(j, 8):
                    e[j, k] = e[j, k] - e[i, j] * e[i, k]
            a, b = left[i] * r, right[i] * r
            for j in range(i + 1, 8):
                left[j] = left[j] - e[i, j] * a
                right[j] = right[j] - e[i, j] * b
            strip_left = jnp.where(sub == i, a, strip_left)
            strip_right = jnp.where(sub == i, b, strip_right)
        m_ref[o : o + 8, :SUB] = strip_left
        m_ref[o : o + 8, SUB:] = strip_right
        if o + 8 < SUB:
            masked = jnp.where(lane >= o + 8, strip_left, 0.0)
            strip = jnp.concatenate([strip_left, strip_right], axis=1)
            update = dot(masked, strip, ((0,), (0,)), lax.Precision.HIGHEST)
            m_ref[o + 8 :, :] = m_ref[o + 8 :, :] - update[o + 8 :, :]


def lead_kernel(place_ref, *refs):
    pieces, (damping_ref, white_ref, inverse_ref, g_ref, m_ref) = refs[:PIECES], refs[PIECES:]
    highest = lax.Precision.HIGHEST
    depth = pieces[0].shape[0]
    same = lax.broadcasted_iota(jnp.int32, (BLOCK, BLOCK), 0) == lax.broadcasted_iota(jnp.int32, (BLOCK, BLOCK), 1)
    gram = jnp.where(same, damping_ref[...], 0.0)
    for i in range(0, PIECES, 4):
        stack = jnp.concatenate([ref[...] for ref in pieces[i : i + 4]])
        gram = gram + dot(stack, stack, ((0,), (0,)), highest)
    g_ref[:, :BLOCK] = gram
    g_ref[:, BLOCK:] = jnp.where(same, 1.0, 0.0)

    def step(p, carry):
        start = pl.multiple_of(p * SUB, SUB)
        m_ref[:, :SUB] = g_ref[pl.ds(start, SUB), pl.ds(start, SUB)]
        m_ref[:, SUB:] = jnp.where(same[:SUB, :SUB], 1.0, 0.0)
        eliminate(m_ref)
        inverse = m_ref[:, SUB:]
        for q in range(BLOCK // SUB):

            @pl.when(p == q)
            def _():
                lo, hi = q * SUB, (q + 1) * SUB
                strip = dot(inverse, g_ref[lo:hi, hi : hi + BLOCK], ((1,), (0,)), highest)
                g_ref[lo:hi, hi : hi + BLOCK] = strip
                if hi < BLOCK:
                    g_ref[hi:BLOCK, hi : hi + BLOCK] = g_ref[hi:BLOCK, hi : hi + BLOCK] - dot(
                        strip[:, : BLOCK - hi], strip, ((0,), (0,)), highest
                    )

        return carry

    lax.fori_loop(0, BLOCK // SUB, step, 0)
    inverse = g_ref[:, BLOCK:]
    inverse_ref[...] = inverse * damping_ref[...]
    pair = split(inverse)
    for i, ref in enumerate(pieces):
        white = dot3(split(ref[...]), pair, ((1,), (1,)))
        part = depth // 4
        for x in range(4):
            start = pl.multiple_of(place_ref[i] * depth + place_ref[PIECES + x] * part, part)
            white_ref[pl.ds(start, part), :] = white[x * part : (x + 1) * part]


def lead_call(pieces, place, damping):
    vmem = pl.BlockSpec(memory_space=pltpu.VMEM)
    rows = PIECES * pieces[0].shape[0]
    return pl.pallas_call(
        lead_kernel,
        out_shape=(jax.ShapeDtypeStruct((rows, BLOCK), jnp.float32), jax.ShapeDtypeStruct((BLOCK, BLOCK), jnp.float32)),
        in_specs=[pl.BlockSpec(memory_space=pltpu.SMEM)] + [vmem] * (PIECES + 1),
        out_specs=(vmem, vmem),
        scratch_shapes=[pltpu.VMEM((BLOCK, 2 * BLOCK), jnp.float32), pltpu.VMEM((SUB, 2 * SUB), jnp.float32)],
        name="lead",
    )(place, *pieces, damping.reshape(1, BLOCK))


def apply_kernel(where_ref, *refs):
    pieces, (columns_ref, white_ref, inverse_ref, out_ref, wh, wl, vh, vl, rh, rl) = refs[:PIECES], refs[PIECES:]
    depth = pieces[0].shape[0]
    t = pl.program_id(0)
    tiles = out_ref.shape[1] // TILE
    is_root = where_ref[0] == 0
    has_panel = where_ref[1] == 0
    white = (wh, wl)

    def put(refs, value, index):
        refs[0][index], refs[1][index] = split(value)

    def get(refs, index=...):
        return refs[0][index], refs[1][index]

    def put_rows(value, columns):
        for k in range(PIECES):
            start = pl.multiple_of(where_ref[2 + k] * depth, depth)
            chunk = slice(k * depth, (k + 1) * depth)
            rh[pl.ds(start, depth), columns] = value[0][chunk]
            rl[pl.ds(start, depth), columns] = value[1][chunk]

    @pl.when(t == 0)
    def _():
        put(white, white_ref[...], ...)

    @pl.when(t < tiles)
    def _():
        here = pl.ds(pl.multiple_of(t * TILE, TILE), TILE)
        in_panel = has_panel & (t * TILE < BLOCK)

        @pl.when(jnp.logical_not(in_panel))
        def _():
            block = columns_ref[...]
            v = split(dot3(get(white), split(block), ((0,), (0,))))
            vh[:, here], vl[:, here] = v
            put_rows(split(block - dot3(get(white), v, ((1,), (0,)))), here)

        @pl.when(in_panel)
        def _():
            row = lax.broadcasted_iota(jnp.int32, (BLOCK, TILE), 0)
            column = lax.broadcasted_iota(jnp.int32, (BLOCK, TILE), 1) + t * TILE
            vh[:, here], vl[:, here] = split(jnp.where(row == column, -1.0, 0.0))
            put_rows((wh[:, here], wl[:, here]), here)

    @pl.when(t >= tiles)
    def _():
        rows = jnp.concatenate([ref[...] for ref in pieces])
        out_ref[...] = dot3(split(rows), get((rh, rl)), ((0,), (0,)))

    for i in range(BLOCK // TILE):

        @pl.when((t == tiles + i) & is_root)
        def _():
            scaled = split(inverse_ref[:, i * TILE : (i + 1) * TILE])
            out_ref[...] = out_ref[...] - dot3(scaled, get((vh, vl)), ((0,), (0,)))


def apply_call(where, pieces, columns, white, inverse):
    depth, size = columns.shape
    tiles = size // TILE
    bf16 = jnp.bfloat16
    grid_spec = pltpu.PrefetchScalarGridSpec(
        num_scalar_prefetch=1,
        grid=(2 * tiles,),
        in_specs=[
            pl.BlockSpec((depth // PIECES, TILE), lambda t, w: (0, jnp.maximum(t - tiles, 0)))
            for _ in range(PIECES)
        ]
        + [
            pl.BlockSpec((depth, TILE), lambda t, w: (0, jnp.minimum(t, tiles - 1))),
            pl.BlockSpec((depth, BLOCK), lambda t, w: (0, 0)),
            pl.BlockSpec((BLOCK, BLOCK), lambda t, w: (0, 0)),
        ],
        out_specs=pl.BlockSpec((TILE, size), lambda t, w: (jnp.maximum(t - tiles, 0), 0)),
        scratch_shapes=[pltpu.VMEM((depth, BLOCK), bf16)] * 2
        + [pltpu.VMEM((BLOCK, size), bf16)] * 2
        + [pltpu.VMEM((depth, size), bf16)] * 2,
    )
    return pl.pallas_call(
        apply_kernel, grid_spec=grid_spec, out_shape=jax.ShapeDtypeStruct((size, size), jnp.float32), name="apply"
    )(where, *pieces, columns, white, inverse)


def per_device(design, damping):
    row = lax.axis_index(ROW)
    col = lax.axis_index(COL)
    quarter = (lax.axis_index("x") + 4 - jnp.array(LEAD_SHIFTS, jnp.int32)) & 3
    place = jnp.concatenate([(places(LEAD_SHIFTS) + col) & 7, quarter]).astype(jnp.int32)
    slots = inverse_of((places(ROW_SHIFTS) + col) & 7)
    where = jnp.concatenate([jnp.stack([row, col]), slots]).astype(jnp.int32)
    columns = lax.all_gather(scatter_columns(design), ("y", "x"), tiled=True)
    lead = spread_lead(design, row == 0)
    rows = gather_rows(design)
    white, inverse = lead_call(lead, place, damping)
    return apply_call(where, rows, columns, white, inverse)


def solution(mesh):
    fine = Mesh(mesh.devices.reshape(SIZES), AXES)
    return jax.shard_map(per_device, mesh=fine, in_specs=(P(COL, ROW), P()), out_specs=P(ROW, COL), check_vma=False)
```

```python
import functools
import itertools

import jax
import jax.numpy as jnp
from jax import lax
from jax.experimental import pallas as pl
from jax.experimental.pallas import tpu as pltpu
from jax.sharding import Mesh
from jax.sharding import PartitionSpec as P


BLOCK = 512
SUB = 128
TILE = 256
PIECES = 8
LEAD_SHIFTS = (0, 1, 3, 2)
ROW_SHIFTS = (0, 1, 2, 3)
AXES = ("zh", "y", "x", "zl", "core")
SIZES = (2, 4, 4, 4, 2)
ROW = ("zh", "y", "x")
COL = ("zl", "core")


def device_id(zh, y, x, zl, core):
    return (((zh * 4 + y) * 4 + x) * 4 + zl) * 2 + core


def ring(n, shift):
    return [(i, (i + shift) % n) for i in range(n)]


def permute_rows(value, moves):
    columns = [(zl, core) for zl in range(4) for core in range(2)]
    values = value if isinstance(value, list) else [value] * len(moves)
    return [
        lax.ppermute(values[i], AXES, [(device_id(*s, *c), device_id(*t, *c)) for s, t in move for c in columns])
        for i, move in enumerate(moves)
    ]


def total(values):
    return functools.reduce(jnp.add, values)


def spread_lead(design, is_root):
    quarters = jnp.split(jnp.where(is_root, design[:, :BLOCK], 0.0), 4)
    others = (1, 3, 2)
    mine = quarters[0] + total(permute_rows([quarters[x] for x in others], [[((0, 0, 0), (0, 0, x))] for x in others]))
    mine = mine + total(permute_rows(mine, [[((0, 0, x), (0, y, x)) for x in range(4)] for y in others]))
    mine = mine + total(permute_rows(mine, [[((0, y, x), (1, y, x)) for y in range(4) for x in range(4)]]))
    mine = jnp.concatenate([mine] + [lax.ppermute(mine, "x", ring(4, k)) for k in LEAD_SHIFTS[1:]])
    line = [mine]
    for k in LEAD_SHIFTS[1:]:
        pairs = []
        for y, x, z, core in itertools.product(range(4), range(4), range(8), range(2)):
            to = (z + (-1 if k == 3 else -2 if k == 2 and core else k)) % 8
            pairs.append((device_id(z // 4, y, x, z % 4, core), device_id(to // 4, y, x, to % 4, core)))
        line.append(lax.ppermute(mine, AXES, pairs))
    return swap_cores(line)


def swap_cores(line):
    return line + [lax.ppermute(piece, "core", ring(2, 1)) for piece in line]


def gather_rows(design):
    return swap_cores([design] + [lax.ppermute(design, "zl", ring(4, k)) for k in ROW_SHIFTS[1:]])


def places(shifts):
    zl, core = lax.axis_index("zl"), lax.axis_index("core")
    chip = (zl + 4 - jnp.array(shifts, jnp.int32)) & 3
    return jnp.concatenate([2 * chip + core, 2 * chip + 1 - core])


def inverse_of(place):
    index = jnp.arange(PIECES, dtype=jnp.int32)
    return jnp.sum(jnp.where(place[None, :] == index[:, None], index[None, :], 0), axis=1)


def scatter_columns(design):
    halves = jnp.split(design, 2)
    planes = []
    for j in range(2):
        pairs = []
        for c, k in itertools.product(range(8), range(8)):
            p = (2 * (k + c) + j) % 16
            pairs.append((device_id(0, c // 4, c % 4, k // 2, k % 2), device_id(0, p // 4, p % 4, k // 2, k % 2)))
        planes.append(lax.ppermute(halves[j], AXES, pairs))
    mine = planes[0] + planes[1]
    lines = []
    for zh in range(2):
        pairs = []
        for p, k in itertools.product(range(16), range(8)):
            c = (p // 2 - k) % 8
            pairs.append((device_id(0, p // 4, p % 4, k // 2, k % 2), device_id(zh, p // 4, p % 4, c // 2, c % 2)))
        lines.append(lax.ppermute(mine, AXES, pairs))
    return lines[0] + lines[1]


def dot(a, b, dims, precision=None):
    return lax.dot_general(a, b, (dims, ((), ())), precision=precision, preferred_element_type=jnp.float32)


def split(a):
    high = a.astype(jnp.bfloat16)
    return high, (a - high.astype(jnp.float32)).astype(jnp.bfloat16)


def dot3(a, b, dims):
    return dot(a[0], b[0], dims) + (dot(a[0], b[1], dims) + dot(a[1], b[0], dims))


def parts(a):
    first = a.astype(jnp.bfloat16).astype(jnp.float32)
    rest = a - first
    second = rest.astype(jnp.bfloat16).astype(jnp.float32)
    return first, second, rest - second


def rank8(a, b):
    a1, a2, a3 = parts(a)
    b1, b2, b3 = parts(b)
    left = jnp.concatenate([a1, a1, a2, a2, a1, a3]).astype(jnp.bfloat16)
    right = jnp.concatenate([b1, b2, b1, b2, b3, b1]).astype(jnp.bfloat16)
    return dot(left, right, ((0,), (0,)))


def eliminate(m_ref):
    lane = lax.broadcasted_iota(jnp.int32, (8, SUB), 1)
    sub = lax.broadcasted_iota(jnp.int32, (8, SUB), 0)

    def entry(row, column):
        return jnp.broadcast_to(row[:, column : column + 1], (8, SUB))

    def load(o):
        return [
            [jnp.broadcast_to(m_ref[o + i : o + i + 1, h * SUB : (h + 1) * SUB], (8, SUB)) for i in range(8)]
            for h in range(2)
        ]

    def stacked(rows):
        strip = rows[7]
        for i in range(7):
            strip = jnp.where(sub == i, rows[i], strip)
        return strip

    left, right = load(0)
    for o in range(0, SUB, 8):
        e = {(i, j): entry(left[i], o + j) for i in range(8) for j in range(i, 8)}
        for i in range(8):
            r = lax.rsqrt(e[i, i])
            for j in range(i + 1, 8):
                e[i, j] = e[i, j] * r
            for j in range(i + 1, 8):
                for k in range(j, 8):
                    e[j, k] = e[j, k] - e[i, j] * e[i, k]
            left[i], right[i] = left[i] * r, right[i] * r
            for j in range(i + 1, 8):
                left[j] = left[j] - e[i, j] * left[i]
                right[j] = right[j] - e[i, j] * right[i]
        strip_left, strip_right = stacked(left), stacked(right)
        m_ref[o : o + 8, :SUB] = strip_left
        m_ref[o : o + 8, SUB:] = strip_right
        n = o + 8
        if n < SUB:
            next_left, next_right = load(n)
            for k in range(8):
                for i in range(8):
                    u = entry(left[i], n + k)
                    next_left[k] = next_left[k] - u * left[i]
                    next_right[k] = next_right[k] - u * right[i]
            left, right = next_left, next_right
        if n + 8 < SUB:
            masked = jnp.where(lane >= n + 8, strip_left, 0.0)
            update = rank8(masked, jnp.concatenate([strip_left, strip_right], axis=1))
            m_ref[n + 8 :, :] = m_ref[n + 8 :, :] - update[n + 8 :, :]


def lead_kernel(place_ref, *refs):
    pieces, (damping_ref, white_ref, inverse_ref, g_ref, m_ref) = refs[:PIECES], refs[PIECES:]
    highest = lax.Precision.HIGHEST
    depth = pieces[0].shape[0]
    same = lax.broadcasted_iota(jnp.int32, (BLOCK, BLOCK), 0) == lax.broadcasted_iota(jnp.int32, (BLOCK, BLOCK), 1)
    gram = jnp.where(same, damping_ref[...], 0.0)
    for i in range(0, PIECES, 4):
        stack = jnp.concatenate([ref[...] for ref in pieces[i : i + 4]])
        gram = gram + dot(stack, stack, ((0,), (0,)), highest)
    g_ref[:, :BLOCK] = gram
    g_ref[:, BLOCK:] = jnp.where(same, 1.0, 0.0)

    def step(p, carry):
        start = pl.multiple_of(p * SUB, SUB)
        m_ref[:, :SUB] = g_ref[pl.ds(start, SUB), pl.ds(start, SUB)]
        m_ref[:, SUB:] = jnp.where(same[:SUB, :SUB], 1.0, 0.0)
        eliminate(m_ref)
        inverse = m_ref[:, SUB:]
        for q in range(BLOCK // SUB):

            @pl.when(p == q)
            def _():
                lo, hi = q * SUB, (q + 1) * SUB
                strip = dot(inverse, g_ref[lo:hi, hi : hi + BLOCK], ((1,), (0,)), highest)
                g_ref[lo:hi, hi : hi + BLOCK] = strip
                if hi < BLOCK:
                    g_ref[hi:BLOCK, hi : hi + BLOCK] = g_ref[hi:BLOCK, hi : hi + BLOCK] - dot(
                        strip[:, : BLOCK - hi], strip, ((0,), (0,)), highest
                    )

        return carry

    lax.fori_loop(0, BLOCK // SUB, step, 0)
    inverse = g_ref[:, BLOCK:]
    inverse_ref[...] = inverse * damping_ref[...]
    pair = split(inverse)
    for i, ref in enumerate(pieces):
        white = dot3(split(ref[...]), pair, ((1,), (1,)))
        part = depth // 4
        for x in range(4):
            start = pl.multiple_of(place_ref[i] * depth + place_ref[PIECES + x] * part, part)
            white_ref[pl.ds(start, part), :] = white[x * part : (x + 1) * part]


def lead_call(pieces, place, damping):
    vmem = pl.BlockSpec(memory_space=pltpu.VMEM)
    rows = PIECES * pieces[0].shape[0]
    return pl.pallas_call(
        lead_kernel,
        out_shape=(jax.ShapeDtypeStruct((rows, BLOCK), jnp.float32), jax.ShapeDtypeStruct((BLOCK, BLOCK), jnp.float32)),
        in_specs=[pl.BlockSpec(memory_space=pltpu.SMEM)] + [vmem] * (PIECES + 1),
        out_specs=(vmem, vmem),
        scratch_shapes=[pltpu.VMEM((BLOCK, 2 * BLOCK), jnp.float32), pltpu.VMEM((SUB, 2 * SUB), jnp.float32)],
        name="lead",
    )(place, *pieces, damping.reshape(1, BLOCK))


def apply_kernel(where_ref, *refs):
    pieces, (columns_ref, white_ref, inverse_ref, out_ref, wh, wl, vh, vl, rh, rl) = refs[:PIECES], refs[PIECES:]
    depth = pieces[0].shape[0]
    t = pl.program_id(0)
    tiles = out_ref.shape[1] // TILE
    is_root = where_ref[0] == 0
    has_panel = where_ref[1] == 0
    white = (wh, wl)

    def put(refs, value, index):
        refs[0][index], refs[1][index] = split(value)

    def get(refs, index=...):
        return refs[0][index], refs[1][index]

    def put_rows(value, columns):
        for k in range(PIECES):
            start = pl.multiple_of(where_ref[2 + k] * depth, depth)
            chunk = slice(k * depth, (k + 1) * depth)
            rh[pl.ds(start, depth), columns] = value[0][chunk]
            rl[pl.ds(start, depth), columns] = value[1][chunk]

    @pl.when(t == 0)
    def _():
        put(white, white_ref[...], ...)

    @pl.when(t < tiles)
    def _():
        here = pl.ds(pl.multiple_of(t * TILE, TILE), TILE)
        in_panel = has_panel & (t * TILE < BLOCK)

        @pl.when(jnp.logical_not(in_panel))
        def _():
            block = columns_ref[...]
            v = split(dot3(get(white), split(block), ((0,), (0,))))
            vh[:, here], vl[:, here] = v
            put_rows(split(block - dot3(get(white), v, ((1,), (0,)))), here)

        @pl.when(in_panel)
        def _():
            row = lax.broadcasted_iota(jnp.int32, (BLOCK, TILE), 0)
            column = lax.broadcasted_iota(jnp.int32, (BLOCK, TILE), 1) + t * TILE
            vh[:, here], vl[:, here] = split(jnp.where(row == column, -1.0, 0.0))
            put_rows((wh[:, here], wl[:, here]), here)

    @pl.when(t >= tiles)
    def _():
        rows = jnp.concatenate([ref[...] for ref in pieces])
        out_ref[...] = dot3(split(rows), get((rh, rl)), ((0,), (0,)))

    for i in range(BLOCK // TILE):

        @pl.when((t == tiles + i) & is_root)
        def _():
            scaled = split(inverse_ref[:, i * TILE : (i + 1) * TILE])
            out_ref[...] = out_ref[...] - dot3(scaled, get((vh, vl)), ((0,), (0,)))


def apply_call(where, pieces, columns, white, inverse):
    depth, size = columns.shape
    tiles = size // TILE
    bf16 = jnp.bfloat16
    grid_spec = pltpu.PrefetchScalarGridSpec(
        num_scalar_prefetch=1,
        grid=(2 * tiles,),
        in_specs=[
            pl.BlockSpec((depth // PIECES, TILE), lambda t, w: (0, jnp.maximum(t - tiles, 0)))
            for _ in range(PIECES)
        ]
        + [
            pl.BlockSpec((depth, TILE), lambda t, w: (0, jnp.minimum(t, tiles - 1))),
            pl.BlockSpec((depth, BLOCK), lambda t, w: (0, 0)),
            pl.BlockSpec((BLOCK, BLOCK), lambda t, w: (0, 0)),
        ],
        out_specs=pl.BlockSpec((TILE, size), lambda t, w: (jnp.maximum(t - tiles, 0), 0)),
        scratch_shapes=[pltpu.VMEM((depth, BLOCK), bf16)] * 2
        + [pltpu.VMEM((BLOCK, size), bf16)] * 2
        + [pltpu.VMEM((depth, size), bf16)] * 2,
    )
    return pl.pallas_call(
        apply_kernel, grid_spec=grid_spec, out_shape=jax.ShapeDtypeStruct((size, size), jnp.float32), name="apply"
    )(where, *pieces, columns, white, inverse)


def per_device(design, damping):
    row = lax.axis_index(ROW)
    col = lax.axis_index(COL)
    quarter = (lax.axis_index("x") + 4 - jnp.array(LEAD_SHIFTS, jnp.int32)) & 3
    place = jnp.concatenate([(places(LEAD_SHIFTS) + col) & 7, quarter]).astype(jnp.int32)
    slots = inverse_of((places(ROW_SHIFTS) + col) & 7)
    where = jnp.concatenate([jnp.stack([row, col]), slots]).astype(jnp.int32)
    columns = lax.all_gather(scatter_columns(design), ("y", "x"), tiled=True)
    lead = spread_lead(design, row == 0)
    rows = gather_rows(design)
    white, inverse = lead_call(lead, place, damping)
    return apply_call(where, rows, columns, white, inverse)


def solution(mesh):
    fine = Mesh(mesh.devices.reshape(SIZES), AXES)
    return jax.shard_map(per_device, mesh=fine, in_specs=(P(COL, ROW), P()), out_specs=P(ROW, COL), check_vma=False)
```

```python
import functools
import itertools

import jax
import jax.numpy as jnp
from jax import lax
from jax.experimental import pallas as pl
from jax.experimental.pallas import tpu as pltpu
from jax.sharding import Mesh
from jax.sharding import PartitionSpec as P


BLOCK = 512
SUB = 128
TILE = 512
PIECES = 8
PLACE = 2 + PIECES
LEAD_SHIFTS = (0, 1, 3, 2)
ROW_SHIFTS = (0, 1, 2, 3)
AXES = ("zh", "y", "x", "zl", "core")
SIZES = (2, 4, 4, 4, 2)
ROW = ("zh", "y", "x")
COL = ("zl", "core")


def device_id(zh, y, x, zl, core):
    return (((zh * 4 + y) * 4 + x) * 4 + zl) * 2 + core


def ring(n, shift):
    return [(i, (i + shift) % n) for i in range(n)]


def permute_rows(value, moves):
    columns = [(zl, core) for zl in range(4) for core in range(2)]
    values = value if isinstance(value, list) else [value] * len(moves)
    return [
        lax.ppermute(values[i], AXES, [(device_id(*s, *c), device_id(*t, *c)) for s, t in move for c in columns])
        for i, move in enumerate(moves)
    ]


def total(values):
    return functools.reduce(jnp.add, values)


def spread_lead(design, is_root):
    quarters = jnp.split(jnp.where(is_root, design[:, :BLOCK], 0.0), 4)
    others = (1, 3, 2)
    mine = quarters[0] + total(permute_rows([quarters[x] for x in others], [[((0, 0, 0), (0, 0, x))] for x in others]))
    mine = mine + total(permute_rows(mine, [[((0, 0, x), (0, y, x)) for x in range(4)] for y in others]))
    mine = mine + total(permute_rows(mine, [[((0, y, x), (1, y, x)) for y in range(4) for x in range(4)]]))
    mine = jnp.concatenate([mine] + [lax.ppermute(mine, "x", ring(4, k)) for k in LEAD_SHIFTS[1:]])
    line = [mine]
    for k in LEAD_SHIFTS[1:]:
        pairs = []
        for y, x, z, core in itertools.product(range(4), range(4), range(8), range(2)):
            to = (z + (-1 if k == 3 else -2 if k == 2 and core else k)) % 8
            pairs.append((device_id(z // 4, y, x, z % 4, core), device_id(to // 4, y, x, to % 4, core)))
        line.append(lax.ppermute(mine, AXES, pairs))
    return swap_cores(line)


def swap_cores(line):
    return line + [lax.ppermute(piece, "core", ring(2, 1)) for piece in line]


def gather_rows(design):
    return swap_cores([design] + [lax.ppermute(design, "zl", ring(4, k)) for k in ROW_SHIFTS[1:]])


def places(shifts):
    zl, core = lax.axis_index("zl"), lax.axis_index("core")
    chip = (zl + 4 - jnp.array(shifts, jnp.int32)) & 3
    return jnp.concatenate([2 * chip + core, 2 * chip + 1 - core])


def inverse_of(place):
    index = jnp.arange(PIECES, dtype=jnp.int32)
    return jnp.sum(jnp.where(place[None, :] == index[:, None], index[None, :], 0), axis=1)


def scatter_columns(design):
    halves = jnp.split(design, 2)
    planes = []
    for j in range(2):
        pairs = []
        for c, k in itertools.product(range(8), range(8)):
            p = (2 * (k + c) + j) % 16
            pairs.append((device_id(0, c // 4, c % 4, k // 2, k % 2), device_id(0, p // 4, p % 4, k // 2, k % 2)))
        planes.append(lax.ppermute(halves[j], AXES, pairs))
    mine = planes[0] + planes[1]
    lines = []
    for zh in range(2):
        pairs = []
        for p, k in itertools.product(range(16), range(8)):
            c = (p // 2 - k) % 8
            pairs.append((device_id(0, p // 4, p % 4, k // 2, k % 2), device_id(zh, p // 4, p % 4, c // 2, c % 2)))
        lines.append(lax.ppermute(mine, AXES, pairs))
    return lines[0] + lines[1]


def dot(a, b, dims, precision=None):
    return lax.dot_general(a, b, (dims, ((), ())), precision=precision, preferred_element_type=jnp.float32)


def split(a):
    high = a.astype(jnp.bfloat16)
    return high, (a - high.astype(jnp.float32)).astype(jnp.bfloat16)


def dot3(a, b, dims):
    return dot(a[0], b[0], dims) + (dot(a[0], b[1], dims) + dot(a[1], b[0], dims))


def parts(a):
    first = a.astype(jnp.bfloat16).astype(jnp.float32)
    rest = a - first
    second = rest.astype(jnp.bfloat16).astype(jnp.float32)
    return first, second, rest - second


def rank8(a, b):
    a1, a2, a3 = parts(a)
    b1, b2, b3 = parts(b)
    left = jnp.concatenate([a1, a1, a2, a2, a1, a3]).astype(jnp.bfloat16)
    right = jnp.concatenate([b1, b2, b1, b2, b3, b1]).astype(jnp.bfloat16)
    return dot(left, right, ((0,), (0,)))


def eliminate(m_ref):
    lane = lax.broadcasted_iota(jnp.int32, (8, SUB), 1)
    sub = lax.broadcasted_iota(jnp.int32, (8, SUB), 0)

    def entry(row, column):
        return jnp.broadcast_to(row[:, column : column + 1], (8, SUB))

    def load(o):
        return [
            [jnp.broadcast_to(m_ref[o + i : o + i + 1, h * SUB : (h + 1) * SUB], (8, SUB)) for i in range(8)]
            for h in range(2)
        ]

    def stacked(rows):
        strip = rows[7]
        for i in range(7):
            strip = jnp.where(sub == i, rows[i], strip)
        return strip

    left, right = load(0)
    for o in range(0, SUB, 8):
        e = {(i, j): entry(left[i], o + j) for i in range(8) for j in range(i, 8)}
        for i in range(8):
            r = lax.rsqrt(e[i, i])
            for j in range(i + 1, 8):
                e[i, j] = e[i, j] * r
            for j in range(i + 1, 8):
                for k in range(j, 8):
                    e[j, k] = e[j, k] - e[i, j] * e[i, k]
            left[i], right[i] = left[i] * r, right[i] * r
            for j in range(i + 1, 8):
                left[j] = left[j] - e[i, j] * left[i]
                right[j] = right[j] - e[i, j] * right[i]
        strip_left, strip_right = stacked(left), stacked(right)
        m_ref[o : o + 8, :SUB] = strip_left
        m_ref[o : o + 8, SUB:] = strip_right
        n = o + 8
        if n < SUB:
            next_left, next_right = load(n)
            for k in range(8):
                for i in range(8):
                    u = entry(left[i], n + k)
                    next_left[k] = next_left[k] - u * left[i]
                    next_right[k] = next_right[k] - u * right[i]
            left, right = next_left, next_right
        if n + 8 < SUB:
            masked = jnp.where(lane >= n + 8, strip_left, 0.0)
            update = rank8(masked, jnp.concatenate([strip_left, strip_right], axis=1))
            m_ref[n + 8 :, :] = m_ref[n + 8 :, :] - update[n + 8 :, :]


def lead_kernel(where_ref, *refs):
    pieces, (damping_ref, white_ref, inverse_ref, g_ref, m_ref, lead_ref, lh_ref, ll_ref) = refs[:PIECES], refs[PIECES:]
    highest = lax.Precision.HIGHEST
    depth = pieces[0].shape[0]
    same = lax.broadcasted_iota(jnp.int32, (BLOCK, BLOCK), 0) == lax.broadcasted_iota(jnp.int32, (BLOCK, BLOCK), 1)
    for i, ref in enumerate(pieces):
        part = depth // 4
        for x in range(4):
            start = pl.multiple_of(where_ref[PLACE + i] * depth + where_ref[PLACE + PIECES + x] * part, part)
            lead_ref[pl.ds(start, part), :] = ref[x * part : (x + 1) * part]
    g_ref[:, :BLOCK] = jnp.where(same, damping_ref[...], 0.0)
    g_ref[:, BLOCK:] = jnp.where(same, 1.0, 0.0)

    def accumulate(i, carry):
        chunk = lead_ref[pl.ds(pl.multiple_of(i * BLOCK, BLOCK), BLOCK), :]
        g_ref[:, :BLOCK] += dot(chunk, chunk, ((0,), (0,)), highest)
        lh_ref[pl.ds(pl.multiple_of(i * BLOCK, BLOCK), BLOCK), :], ll_ref[pl.ds(pl.multiple_of(i * BLOCK, BLOCK), BLOCK), :] = split(chunk)
        return carry

    lax.fori_loop(0, lead_ref.shape[0] // BLOCK, accumulate, 0)

    def whiten(p):
        here = pl.ds(pl.multiple_of(p * SUB, SUB), SUB)
        white_ref[:, here] = dot3((lh_ref[...], ll_ref[...]), split(g_ref[here, BLOCK:]), ((1,), (1,)))

    def step(p, carry):
        start = pl.multiple_of(p * SUB, SUB)
        m_ref[:, :SUB] = g_ref[pl.ds(start, SUB), pl.ds(start, SUB)]
        m_ref[:, SUB:] = jnp.where(same[:SUB, :SUB], 1.0, 0.0)
        whiten(jnp.maximum(p - 1, 0))
        eliminate(m_ref)
        inverse = m_ref[:, SUB:]
        for q in range(BLOCK // SUB):

            @pl.when(p == q)
            def _():
                lo, hi = q * SUB, (q + 1) * SUB
                strip = dot(inverse, g_ref[lo:hi, hi : hi + BLOCK], ((1,), (0,)), highest)
                g_ref[lo:hi, hi : hi + BLOCK] = strip
                if hi < BLOCK:
                    g_ref[hi:BLOCK, hi : hi + BLOCK] = g_ref[hi:BLOCK, hi : hi + BLOCK] - dot(
                        strip[:, : BLOCK - hi], strip, ((0,), (0,)), highest
                    )

        return carry

    lax.fori_loop(0, BLOCK // SUB, step, 0)
    whiten(BLOCK // SUB - 1)
    inverse_ref[...] = g_ref[:, BLOCK:] * damping_ref[...]


def lead_call(pieces, where, damping):
    vmem = pl.BlockSpec(memory_space=pltpu.VMEM)
    rows = PIECES * pieces[0].shape[0]
    return pl.pallas_call(
        lead_kernel,
        out_shape=(jax.ShapeDtypeStruct((rows, BLOCK), jnp.float32), jax.ShapeDtypeStruct((BLOCK, BLOCK), jnp.float32)),
        in_specs=[pl.BlockSpec(memory_space=pltpu.SMEM)] + [vmem] * (PIECES + 1),
        out_specs=(vmem, vmem),
        scratch_shapes=[
            pltpu.VMEM((BLOCK, 2 * BLOCK), jnp.float32),
            pltpu.VMEM((SUB, 2 * SUB), jnp.float32),
            pltpu.VMEM((rows, BLOCK), jnp.float32),
        ]
        + [pltpu.VMEM((rows, BLOCK), jnp.bfloat16)] * 2,
        name="lead",
    )(where, *pieces, damping.reshape(1, BLOCK))


def apply_kernel(where_ref, *refs):
    pieces, (columns_ref, white_ref, inverse_ref, out_ref, wh, wl, vh, vl, rh, rl) = refs[:PIECES], refs[PIECES:]
    depth = pieces[0].shape[0]
    t = pl.program_id(0)
    tiles = out_ref.shape[1] // TILE
    is_root = where_ref[0] == 0
    has_panel = where_ref[1] == 0
    white = (wh, wl)

    def put(refs, value, index):
        refs[0][index], refs[1][index] = split(value)

    def get(refs, index=...):
        return refs[0][index], refs[1][index]

    def put_rows(value, columns):
        for k in range(PIECES):
            start = pl.multiple_of(where_ref[2 + k] * depth, depth)
            chunk = slice(k * depth, (k + 1) * depth)
            rh[pl.ds(start, depth), columns] = value[0][chunk]
            rl[pl.ds(start, depth), columns] = value[1][chunk]

    @pl.when(t == 0)
    def _():
        put(white, white_ref[...], ...)

    @pl.when(t < tiles)
    def _():
        here = pl.ds(pl.multiple_of(t * TILE, TILE), TILE)
        in_panel = has_panel & (t * TILE < BLOCK)

        @pl.when(jnp.logical_not(in_panel))
        def _():
            block = columns_ref[...]
            v = split(dot3(get(white), split(block), ((0,), (0,))))
            vh[:, here], vl[:, here] = v
            put_rows(split(block - dot3(get(white), v, ((1,), (0,)))), here)

        @pl.when(in_panel)
        def _():
            row = lax.broadcasted_iota(jnp.int32, (BLOCK, TILE), 0)
            column = lax.broadcasted_iota(jnp.int32, (BLOCK, TILE), 1) + t * TILE
            vh[:, here], vl[:, here] = split(jnp.where(row == column, -1.0, 0.0))
            put_rows((wh[:, here], wl[:, here]), here)

    @pl.when(t >= tiles)
    def _():
        rows = jnp.concatenate([ref[...] for ref in pieces])
        out_ref[...] = dot3(split(rows), get((rh, rl)), ((0,), (0,)))

    for i in range(BLOCK // TILE):

        @pl.when((t == tiles + i) & is_root)
        def _():
            scaled = split(inverse_ref[:, i * TILE : (i + 1) * TILE])
            out_ref[...] = out_ref[...] - dot3(scaled, get((vh, vl)), ((0,), (0,)))


def apply_call(where, pieces, columns, white, inverse):
    depth, size = columns.shape
    tiles = size // TILE
    bf16 = jnp.bfloat16
    grid_spec = pltpu.PrefetchScalarGridSpec(
        num_scalar_prefetch=1,
        grid=(2 * tiles,),
        in_specs=[
            pl.BlockSpec((depth // PIECES, TILE), lambda t, w: (0, jnp.maximum(t - tiles, 0)))
            for _ in range(PIECES)
        ]
        + [
            pl.BlockSpec((depth, TILE), lambda t, w: (0, jnp.minimum(t, tiles - 1))),
            pl.BlockSpec((depth, BLOCK), lambda t, w: (0, 0)),
            pl.BlockSpec((BLOCK, BLOCK), lambda t, w: (0, 0)),
        ],
        out_specs=pl.BlockSpec((TILE, size), lambda t, w: (jnp.maximum(t - tiles, 0), 0)),
        scratch_shapes=[pltpu.VMEM((depth, BLOCK), bf16)] * 2
        + [pltpu.VMEM((BLOCK, size), bf16)] * 2
        + [pltpu.VMEM((depth, size), bf16)] * 2,
    )
    return pl.pallas_call(
        apply_kernel, grid_spec=grid_spec, out_shape=jax.ShapeDtypeStruct((size, size), jnp.float32), name="apply"
    )(where, *pieces, columns, white, inverse)


def per_device(design, damping):
    row = lax.axis_index(ROW)
    col = lax.axis_index(COL)
    quarter = (lax.axis_index("x") + 4 - jnp.array(LEAD_SHIFTS, jnp.int32)) & 3
    slots = inverse_of((places(ROW_SHIFTS) + col) & 7)
    place = (places(LEAD_SHIFTS) + col) & 7
    where = jnp.concatenate([jnp.stack([row, col]), slots, place, quarter]).astype(jnp.int32)
    columns = lax.all_gather(scatter_columns(design), ("y", "x"), tiled=True)
    lead = spread_lead(design, row == 0)
    rows = gather_rows(design)
    white, inverse = lead_call(lead, where, damping)
    return apply_call(where, rows, columns, white, inverse)


def solution(mesh):
    fine = Mesh(mesh.devices.reshape(SIZES), AXES)
    return jax.shard_map(per_device, mesh=fine, in_specs=(P(COL, ROW), P()), out_specs=P(ROW, COL), check_vma=False)
```

```python
import functools
import itertools

import jax
import jax.numpy as jnp
from jax import lax
from jax.experimental import pallas as pl
from jax.experimental.pallas import tpu as pltpu
from jax.sharding import Mesh
from jax.sharding import PartitionSpec as P


BLOCK = 512
SUB = 128
TILE = 512
PIECES = 8
PLACE = 2 + PIECES
LEAD_SHIFTS = (0, 1, 3, 2)
ROW_SHIFTS = (0, 1, 2, 3)
AXES = ("zh", "y", "x", "zl", "core")
SIZES = (2, 4, 4, 4, 2)
ROW = ("zh", "y", "x")
COL = ("zl", "core")


def device_id(zh, y, x, zl, core):
    return (((zh * 4 + y) * 4 + x) * 4 + zl) * 2 + core


def ring(n, shift):
    return [(i, (i + shift) % n) for i in range(n)]


def permute_rows(value, moves):
    columns = [(zl, core) for zl in range(4) for core in range(2)]
    values = value if isinstance(value, list) else [value] * len(moves)
    return [
        lax.ppermute(values[i], AXES, [(device_id(*s, *c), device_id(*t, *c)) for s, t in move for c in columns])
        for i, move in enumerate(moves)
    ]


def total(values):
    return functools.reduce(jnp.add, values)


def spread_lead(design, is_root):
    quarters = jnp.split(jnp.where(is_root, design[:, :BLOCK], 0.0), 4)
    others = (1, 3, 2)
    mine = quarters[0] + total(permute_rows([quarters[x] for x in others], [[((0, 0, 0), (0, 0, x))] for x in others]))
    mine = mine + total(permute_rows(mine, [[((0, 0, x), (0, y, x)) for x in range(4)] for y in others]))
    mine = mine + total(permute_rows(mine, [[((0, y, x), (1, y, x)) for y in range(4) for x in range(4)]]))
    mine = jnp.concatenate([mine] + [lax.ppermute(mine, "x", ring(4, k)) for k in LEAD_SHIFTS[1:]])
    line = [mine]
    for k in LEAD_SHIFTS[1:]:
        pairs = []
        for y, x, z, core in itertools.product(range(4), range(4), range(8), range(2)):
            to = (z + (-1 if k == 3 else -2 if k == 2 and core else k)) % 8
            pairs.append((device_id(z // 4, y, x, z % 4, core), device_id(to // 4, y, x, to % 4, core)))
        line.append(lax.ppermute(mine, AXES, pairs))
    return swap_cores(line)


def swap_cores(line):
    return line + [lax.ppermute(piece, "core", ring(2, 1)) for piece in line]


def gather_rows(design):
    return swap_cores([design] + [lax.ppermute(design, "zl", ring(4, k)) for k in ROW_SHIFTS[1:]])


def places(shifts):
    zl, core = lax.axis_index("zl"), lax.axis_index("core")
    chip = (zl + 4 - jnp.array(shifts, jnp.int32)) & 3
    return jnp.concatenate([2 * chip + core, 2 * chip + 1 - core])


def inverse_of(place):
    index = jnp.arange(PIECES, dtype=jnp.int32)
    return jnp.sum(jnp.where(place[None, :] == index[:, None], index[None, :], 0), axis=1)


def scatter_columns(design):
    halves = jnp.split(design, 2)
    planes = []
    for j in range(2):
        pairs = []
        for c, k in itertools.product(range(8), range(8)):
            p = (2 * (k + c) + j) % 16
            pairs.append((device_id(0, c // 4, c % 4, k // 2, k % 2), device_id(0, p // 4, p % 4, k // 2, k % 2)))
        planes.append(lax.ppermute(halves[j], AXES, pairs))
    mine = planes[0] + planes[1]
    lines = []
    for zh in range(2):
        pairs = []
        for p, k in itertools.product(range(16), range(8)):
            c = (p // 2 - k) % 8
            pairs.append((device_id(0, p // 4, p % 4, k // 2, k % 2), device_id(zh, p // 4, p % 4, c // 2, c % 2)))
        lines.append(lax.ppermute(mine, AXES, pairs))
    return lines[0] + lines[1]


def dot(a, b, dims, precision=None):
    return lax.dot_general(a, b, (dims, ((), ())), precision=precision, preferred_element_type=jnp.float32)


def split(a):
    high = a.astype(jnp.bfloat16)
    return high, (a - high.astype(jnp.float32)).astype(jnp.bfloat16)


def dot3(a, b, dims):
    return dot(a[0], b[0], dims) + (dot(a[0], b[1], dims) + dot(a[1], b[0], dims))


def parts(a):
    first = a.astype(jnp.bfloat16).astype(jnp.float32)
    rest = a - first
    second = rest.astype(jnp.bfloat16).astype(jnp.float32)
    return first, second, rest - second


def rank8(a, b):
    a1, a2, a3 = parts(a)
    b1, b2, b3 = parts(b)
    left = jnp.concatenate([a1, a1, a2, a2, a1, a3]).astype(jnp.bfloat16)
    right = jnp.concatenate([b1, b2, b1, b2, b3, b1]).astype(jnp.bfloat16)
    return dot(left, right, ((0,), (0,)))


def eliminate(m_ref):
    lane = lax.broadcasted_iota(jnp.int32, (8, SUB), 1)
    sub = lax.broadcasted_iota(jnp.int32, (8, SUB), 0)

    def entry(row, column):
        return jnp.broadcast_to(row[:, column : column + 1], (8, SUB))

    def load(o):
        return [
            [jnp.broadcast_to(m_ref[o + i : o + i + 1, h * SUB : (h + 1) * SUB], (8, SUB)) for i in range(8)]
            for h in range(2)
        ]

    def stacked(rows):
        strip = rows[7]
        for i in range(7):
            strip = jnp.where(sub == i, rows[i], strip)
        return strip

    left, right = load(0)
    for o in range(0, SUB, 8):
        e = {(i, j): entry(left[i], o + j) for i in range(8) for j in range(i, 8)}
        for i in range(8):
            r = lax.rsqrt(e[i, i])
            for j in range(i + 1, 8):
                e[i, j] = e[i, j] * r
            for j in range(i + 1, 8):
                for k in range(j, 8):
                    e[j, k] = e[j, k] - e[i, j] * e[i, k]
            left[i], right[i] = left[i] * r, right[i] * r
            for j in range(i + 1, 8):
                left[j] = left[j] - e[i, j] * left[i]
                right[j] = right[j] - e[i, j] * right[i]
        strip_left, strip_right = stacked(left), stacked(right)
        m_ref[o : o + 8, :SUB] = strip_left
        m_ref[o : o + 8, SUB:] = strip_right
        n = o + 8
        if n < SUB:
            next_left, next_right = load(n)
            for k in range(8):
                for i in range(8):
                    u = entry(left[i], n + k)
                    next_left[k] = next_left[k] - u * left[i]
                    next_right[k] = next_right[k] - u * right[i]
            left, right = next_left, next_right
        if n + 8 < SUB:
            masked = jnp.where(lane >= n + 8, strip_left, 0.0)
            update = rank8(masked, jnp.concatenate([strip_left, strip_right], axis=1))
            m_ref[n + 8 :, :] = m_ref[n + 8 :, :] - update[n + 8 :, :]


def lead_kernel(where_ref, *refs):
    pieces, (damping_ref, white_ref, inverse_ref, g_ref, m_ref, lead_ref, lh_ref, ll_ref) = refs[:PIECES], refs[PIECES:]
    highest = lax.Precision.HIGHEST
    depth = pieces[0].shape[0]
    same = lax.broadcasted_iota(jnp.int32, (BLOCK, BLOCK), 0) == lax.broadcasted_iota(jnp.int32, (BLOCK, BLOCK), 1)
    for i, ref in enumerate(pieces):
        part = depth // 4
        for x in range(4):
            start = pl.multiple_of(where_ref[PLACE + i] * depth + where_ref[PLACE + PIECES + x] * part, part)
            lead_ref[pl.ds(start, part), :] = ref[x * part : (x + 1) * part]
    g_ref[:, :BLOCK] = jnp.where(same, damping_ref[...], 0.0)
    g_ref[:, BLOCK:] = jnp.where(same, 1.0, 0.0)

    def accumulate(i, carry):
        here = pl.ds(pl.multiple_of(i * BLOCK, BLOCK), BLOCK)
        chunk = lead_ref[here, :]
        for lo in range(0, BLOCK, TILE // 2):
            hi = lo + TILE // 2
            g_ref[lo:hi, lo:BLOCK] += dot(chunk[:, lo:hi], chunk[:, lo:], ((0,), (0,)), highest)
        lh_ref[here, :], ll_ref[here, :] = split(chunk)
        return carry

    lax.fori_loop(0, lead_ref.shape[0] // BLOCK, accumulate, 0)

    def whiten(p):
        here = pl.ds(pl.multiple_of(p * SUB, SUB), SUB)
        white_ref[:, here] = dot3((lh_ref[...], ll_ref[...]), split(g_ref[here, BLOCK:]), ((1,), (1,)))

    def step(p, carry):
        start = pl.multiple_of(p * SUB, SUB)
        m_ref[:, :SUB] = g_ref[pl.ds(start, SUB), pl.ds(start, SUB)]
        m_ref[:, SUB:] = jnp.where(same[:SUB, :SUB], 1.0, 0.0)
        whiten(jnp.maximum(p - 1, 0))
        eliminate(m_ref)
        inverse = m_ref[:, SUB:]
        for q in range(BLOCK // SUB):

            @pl.when(p == q)
            def _():
                lo, hi = q * SUB, (q + 1) * SUB
                strip = dot(inverse, g_ref[lo:hi, hi : hi + BLOCK], ((1,), (0,)), highest)
                g_ref[lo:hi, hi : hi + BLOCK] = strip
                if hi < BLOCK:
                    g_ref[hi:BLOCK, hi : hi + BLOCK] = g_ref[hi:BLOCK, hi : hi + BLOCK] - dot(
                        strip[:, : BLOCK - hi], strip, ((0,), (0,)), highest
                    )

        return carry

    lax.fori_loop(0, BLOCK // SUB, step, 0)
    whiten(BLOCK // SUB - 1)
    inverse_ref[...] = g_ref[:, BLOCK:] * damping_ref[...]


def lead_call(pieces, where, damping):
    vmem = pl.BlockSpec(memory_space=pltpu.VMEM)
    rows = PIECES * pieces[0].shape[0]
    return pl.pallas_call(
        lead_kernel,
        out_shape=(jax.ShapeDtypeStruct((rows, BLOCK), jnp.float32), jax.ShapeDtypeStruct((BLOCK, BLOCK), jnp.float32)),
        in_specs=[pl.BlockSpec(memory_space=pltpu.SMEM)] + [vmem] * (PIECES + 1),
        out_specs=(vmem, vmem),
        scratch_shapes=[
            pltpu.VMEM((BLOCK, 2 * BLOCK), jnp.float32),
            pltpu.VMEM((SUB, 2 * SUB), jnp.float32),
            pltpu.VMEM((rows, BLOCK), jnp.float32),
        ]
        + [pltpu.VMEM((rows, BLOCK), jnp.bfloat16)] * 2,
        name="lead",
    )(where, *pieces, damping.reshape(1, BLOCK))


def apply_kernel(where_ref, *refs):
    pieces, (columns_ref, white_ref, inverse_ref, out_ref, wh, wl, vh, vl, rh, rl) = refs[:PIECES], refs[PIECES:]
    depth = pieces[0].shape[0]
    t = pl.program_id(0)
    tiles = out_ref.shape[1] // TILE
    is_root = where_ref[0] == 0
    has_panel = where_ref[1] == 0
    white = (wh, wl)

    def put(refs, value, index):
        refs[0][index], refs[1][index] = split(value)

    def get(refs, index=...):
        return refs[0][index], refs[1][index]

    def put_rows(value, columns):
        for k in range(PIECES):
            start = pl.multiple_of(where_ref[2 + k] * depth, depth)
            chunk = slice(k * depth, (k + 1) * depth)
            rh[pl.ds(start, depth), columns] = value[0][chunk]
            rl[pl.ds(start, depth), columns] = value[1][chunk]

    @pl.when(t == 0)
    def _():
        put(white, white_ref[...], ...)

    @pl.when(t < tiles)
    def _():
        here = pl.ds(pl.multiple_of(t * TILE, TILE), TILE)
        in_panel = has_panel & (t * TILE < BLOCK)

        @pl.when(jnp.logical_not(in_panel))
        def _():
            block = columns_ref[...]
            v = split(dot3(get(white), split(block), ((0,), (0,))))
            vh[:, here], vl[:, here] = v
            put_rows(split(block - dot3(get(white), v, ((1,), (0,)))), here)

        @pl.when(in_panel)
        def _():
            row = lax.broadcasted_iota(jnp.int32, (BLOCK, TILE), 0)
            column = lax.broadcasted_iota(jnp.int32, (BLOCK, TILE), 1) + t * TILE
            vh[:, here], vl[:, here] = split(jnp.where(row == column, -1.0, 0.0))
            put_rows((wh[:, here], wl[:, here]), here)

    @pl.when(t >= tiles)
    def _():
        rows = jnp.concatenate([ref[...] for ref in pieces])
        out_ref[...] = dot3(split(rows), get((rh, rl)), ((0,), (0,)))

    for i in range(BLOCK // TILE):

        @pl.when((t == tiles + i) & is_root)
        def _():
            scaled = split(inverse_ref[:, i * TILE : (i + 1) * TILE])
            out_ref[...] = out_ref[...] - dot3(scaled, get((vh, vl)), ((0,), (0,)))


def apply_call(where, pieces, columns, white, inverse):
    depth, size = columns.shape
    tiles = size // TILE
    bf16 = jnp.bfloat16
    grid_spec = pltpu.PrefetchScalarGridSpec(
        num_scalar_prefetch=1,
        grid=(2 * tiles,),
        in_specs=[
            pl.BlockSpec((depth // PIECES, TILE), lambda t, w: (0, jnp.maximum(t - tiles, 0)))
            for _ in range(PIECES)
        ]
        + [
            pl.BlockSpec((depth, TILE), lambda t, w: (0, jnp.minimum(t, tiles - 1))),
            pl.BlockSpec((depth, BLOCK), lambda t, w: (0, 0)),
            pl.BlockSpec((BLOCK, BLOCK), lambda t, w: (0, 0)),
        ],
        out_specs=pl.BlockSpec((TILE, size), lambda t, w: (jnp.maximum(t - tiles, 0), 0)),
        scratch_shapes=[pltpu.VMEM((depth, BLOCK), bf16)] * 2
        + [pltpu.VMEM((BLOCK, size), bf16)] * 2
        + [pltpu.VMEM((depth, size), bf16)] * 2,
    )
    return pl.pallas_call(
        apply_kernel, grid_spec=grid_spec, out_shape=jax.ShapeDtypeStruct((size, size), jnp.float32), name="apply"
    )(where, *pieces, columns, white, inverse)


def per_device(design, damping):
    row = lax.axis_index(ROW)
    col = lax.axis_index(COL)
    quarter = (lax.axis_index("x") + 4 - jnp.array(LEAD_SHIFTS, jnp.int32)) & 3
    slots = inverse_of((places(ROW_SHIFTS) + col) & 7)
    place = (places(LEAD_SHIFTS) + col) & 7
    where = jnp.concatenate([jnp.stack([row, col]), slots, place, quarter]).astype(jnp.int32)
    columns = lax.all_gather(scatter_columns(design), ("y", "x"), tiled=True)
    lead = spread_lead(design, row == 0)
    rows = gather_rows(design)
    white, inverse = lead_call(lead, where, damping)
    return apply_call(where, rows, columns, white, inverse)


def solution(mesh):
    fine = Mesh(mesh.devices.reshape(SIZES), AXES)
    return jax.shard_map(per_device, mesh=fine, in_specs=(P(COL, ROW), P()), out_specs=P(ROW, COL), check_vma=False)
```
